768 devices in a mesh: fsdp: 96 (over y_hi, z, core), seq: 8 (over y_lo, x).
Axes of the slice: x: 4, y: 8 (y_hi: 4, y_lo: 2; y = y_hi * 2 + y_lo), z: 12, core: 2. Of those that a mesh axis runs over, the one named last changes fastest.
Arguments:
- query_proj: bfloat16 [96, 1024, 3072], P('fsdp', 'seq'), may hold values from -6 to 6
- key_proj: bfloat16 [96, 1024, 3072], P('fsdp', 'seq'), may hold values from 0 to 5
- value_proj: bfloat16 [96, 1024, 3072], P('fsdp', 'seq'), may hold values from 0 to 5
- filters: float32 [3072, 128], P('fsdp'), may hold values from -8 to 8
Outputs:
- response: bfloat16 [96, 1024, 3072], P('fsdp', 'seq')
The draws below stay inside these ranges and needn't reach their ends.
All inputs are finite; a program needn't handle non-finite values.
Results may differ from the reference program's by a relative error of at most 0.012.
Values may be sent and summed in bfloat16 or wider, within the bound.
No kernel may reach another device: no remote copies, remote signals or barrier semaphores. Data moves between devices by JAX's collectives and lax.ppermute only.
A program may use at most 32 MiB of HBM per device.

```python
import jax
import jax.numpy as jnp
from jax import lax

CH = 3072
TAPS = 128
L = 1024
GENOMES = 96


def draw_filters(key, part):
    first, second, third = jax.random.split(jax.random.fold_in(key, 11), 3)
    spans = jnp.exp(jax.random.uniform(first, (CH, 1), minval=jnp.log(0.5 * TAPS), maxval=jnp.log(4.0 * TAPS)))
    steps = jnp.arange(TAPS, dtype=jnp.float32)[None, :]
    signs = 1.0 - 2.0 * (jnp.arange(TAPS) % 2).astype(jnp.float32)[None, :]
    magnitude = 1.0 + 0.5 * jnp.tanh(jax.random.normal(second, (CH, TAPS)))
    scale = jnp.exp(jax.random.uniform(third, (CH, 1), minval=jnp.log(0.5), maxval=jnp.log(2.0)))
    energy = (1.0 - jnp.exp(-2.0 * TAPS / spans)) / (1.0 - jnp.exp(-2.0 / spans))
    lifted = signs * magnitude * jnp.exp(-steps / spans) * scale / jnp.sqrt(4.33 * energy)
    return (lifted - jnp.roll(lifted, 1, axis=1)).astype(jnp.float32)


def draw_key_proj(key, part):
    first, second = jax.random.split(jax.random.fold_in(key, 23), 2)
    centre = jax.random.uniform(first, (1, 1, CH), minval=2.2, maxval=2.8)
    noise = 0.45 * jnp.clip(jax.random.normal(second, (GENOMES, L, CH)), -4.4, 4.4)
    return (centre + noise).astype(jnp.bfloat16)


def draw_value_proj(key, part):
    first, second = jax.random.split(jax.random.fold_in(key, 37), 2)
    centre = jax.random.uniform(first, (1, 1, CH), minval=2.2, maxval=2.8)
    noise = 0.45 * jnp.clip(jax.random.normal(second, (GENOMES, L, CH)), -4.4, 4.4)
    return (centre + noise).astype(jnp.bfloat16)


def block_scale(own_key, shape, pieces, low, top_value):
    level, own = 1.0, jax.random.fold_in(own_key, 6)
    for dim, blocks in pieces:
        draws = jnp.exp(jax.random.uniform(jax.random.fold_in(own, dim), (blocks,), jnp.float32, low / len(pieces), top_value / len(pieces)))
        level = level * jnp.repeat(draws, shape[dim] // blocks).reshape([-1 if axis == dim else 1 for axis in range(len(shape))])
    return level


def bell_draw(key, extent, scale, limit, cuts=(), held_as=jnp.bfloat16):
    gain = block_scale(key, extent, cuts, -0.22, 0.18) if cuts else 1.0
    result = jax.random.normal(key, extent, jnp.float32) * scale * gain
    return jnp.minimum(jnp.maximum(result, -limit), limit).astype(held_as)


def setup_inputs(seed: int = 0) -> dict:
    streams_of = jax.random.split(jax.random.key(seed), 5)
    return {
        "query_proj": bell_draw(streams_of[0], (GENOMES, L, CH), 1.0, 6.0, ((0, 96), (1, 8))),
        "key_proj": draw_key_proj(jax.random.fold_in(streams_of[4], 71), 0),
        "value_proj": draw_value_proj(jax.random.fold_in(streams_of[4], 71), 0),
        "filters": draw_filters(jax.random.fold_in(streams_of[4], 71), 0),
    }


def causal_filter(padded, taps):
    length = padded.shape[0] - TAPS + 1

    def add_tap(index, total):
        offset = (TAPS - 1 - index).astype(jnp.int32)
        window = lax.dynamic_slice_in_dim(padded, offset, length, 0)
        weight = lax.dynamic_index_in_dim(taps, index.astype(jnp.int32), 1, keepdims=False)
        return total + weight[None, :] * window

    start = jnp.zeros((length, padded.shape[1]), jnp.float32)
    return lax.fori_loop(jnp.int32(0), jnp.int32(TAPS), add_tap, start)


def one_genome(operands):
    query_row, key_row, value_row, taps = operands
    mixed = (key_row.astype(jnp.float32) * value_row.astype(jnp.float32)).astype(jnp.bfloat16)
    padded = jnp.pad(mixed.astype(jnp.float32), ((TAPS - 1, 0), (0, 0)))
    filtered = causal_filter(padded, taps)
    return (query_row.astype(jnp.float32) * filtered).astype(jnp.bfloat16)


def reference(query_proj, key_proj, value_proj, filters):
    def single(items):
        return one_genome((items[0], items[1], items[2], filters))
    return lax.map(single, (query_proj, key_proj, value_proj))
```

```python
import functools

import jax
import jax.numpy as jnp
import numpy as np
from jax import lax
from jax.experimental import pallas as pl
from jax.experimental.pallas import tpu as pltpu
from jax.sharding import PartitionSpec as P

WIRE = jnp.float16
SCALE = 4096.0


def split(x):
    x = np.asarray(x, np.float32)
    hi = x.astype(jnp.bfloat16)
    return hi, (x - hi.astype(np.float32)).astype(jnp.bfloat16)


def transforms(taps):
    n = 2 * taps
    angle = 2 * np.pi * np.outer(np.arange(taps) + 0.5, np.arange(n)) / n
    forward = np.concatenate([np.cos(angle), -np.sin(angle)])
    inverse = np.concatenate([np.cos(angle), -np.sin(angle)]).T[taps:] / taps
    fh, fl = split(forward)
    gh, gl = split(inverse / SCALE)
    return np.concatenate([fh, fl]), np.concatenate([gh, gl])


def rows_of(ref):
    both = jnp.concatenate([ref[0], ref[1]], axis=1)
    return both.reshape(-1, both.shape[-1])


def conv_kernel(prev_ref, cur_ref, query_ref, wh_ref, wl_ref, f_ref, g_ref, out_ref):
    f32 = jnp.float32
    half, taps = f_ref.shape[0] // 2, cur_ref.shape[1]
    dot = functools.partial(jnp.dot, preferred_element_type=f32)
    f = f_ref[...]
    window = jnp.concatenate([prev_ref[0], cur_ref[0]], axis=0)
    x = dot(f, window)
    x = x[:half] + x[half:]
    nt = functools.partial(
        lax.dot_general, dimension_numbers=(((1,), (1,)), ((), ())), preferred_element_type=f32
    )
    h = nt(f[:, :taps], rows_of(wh_ref))
    h = h[:half] + h[half:] + nt(f[:half, :taps], rows_of(wl_ref))
    xr, xi, hr, hi = x[:taps], x[taps:], h[:taps], h[taps:]
    p = jnp.concatenate([xr * hr - xi * hi, xr * hi + xi * hr], axis=0)
    ph = p.astype(jnp.bfloat16)
    plo = (p - ph.astype(f32)).astype(jnp.bfloat16)
    g = g_ref[...]
    y = dot(g, ph)
    y = y[:taps] + y[taps:] + dot(g[:taps], plo)
    out_ref[0] = (query_ref[0].astype(f32) * y).astype(out_ref.dtype)


def filtered_gate(prev, cur, query, coarse, fine, forward, inverse, shards):
    _, rows, channels = cur.shape
    own = channels // coarse.shape[1]
    shard = pl.BlockSpec((2, shards) + coarse.shape[2:], lambda i: (0, i, 0, 0))
    width = own * shards
    block = pl.BlockSpec((1, rows, width), lambda i: (0, 0, i))
    return pl.pallas_call(
        conv_kernel,
        grid=(channels // width,),
        in_specs=[
            block,
            block,
            block,
            shard,
            shard,
            pl.BlockSpec(forward.shape, lambda i: (0, 0)),
            pl.BlockSpec(inverse.shape, lambda i: (0, 0)),
        ],
        out_specs=block,
        out_shape=jax.ShapeDtypeStruct(cur.shape, jnp.bfloat16),
        name="filtered_gate",
    )(prev, cur, query, coarse, fine, forward, inverse)


def per_device(query_proj, key_proj, value_proj, filters):
    f32 = jnp.float32
    peers = lax.axis_size("fsdp")
    own, taps = filters.shape
    halves = (filters * SCALE).astype(WIRE).reshape(1, 2, own // 2, taps)
    send = jnp.broadcast_to(halves, (peers // 2, 2, own // 2, taps)).reshape(peers, own // 2, taps)
    got = lax.all_to_all(send, "fsdp", 0, 0, tiled=True)
    pairs = [[2 * i, 2 * i + 1] for i in range(peers // 2)]
    both = lax.all_to_all(
        jnp.broadcast_to(got[None], (2,) + got.shape), "fsdp", 0, 0, axis_index_groups=pairs, tiled=True
    )
    mixed = (key_proj.astype(f32) * value_proj.astype(f32)).astype(jnp.bfloat16)
    steps = lax.axis_size("seq")
    earlier = lax.ppermute(mixed, "seq", [(i, i + 1) for i in range(steps - 1)])
    forward, inverse = transforms(taps)
    both = both.reshape(2, peers, own // 2, taps).astype(f32)
    coarse = both.astype(jnp.bfloat16)
    fine = (both - coarse.astype(f32)).astype(jnp.bfloat16)
    return filtered_gate(earlier, mixed, query_proj, coarse, fine, forward, inverse, 16)


def solution(mesh):
    rows = P("fsdp", "seq", None)
    return jax.shard_map(
        per_device,
        mesh=mesh,
        in_specs=(rows, rows, rows, P("fsdp", None)),
        out_specs=rows,
        check_vma=False,
    )
```

```python
import functools

import jax
import jax.numpy as jnp
import numpy as np
from jax import lax
from jax.experimental import pallas as pl
from jax.sharding import PartitionSpec as P

WIRE = jnp.float16
SCALE = 4096.0


def split(x):
    x = np.asarray(x, np.float32)
    hi = x.astype(jnp.bfloat16)
    return hi, (x - hi.astype(np.float32)).astype(jnp.bfloat16)


def transforms(taps):
    n = 2 * taps
    angle = 2 * np.pi * np.outer(np.arange(taps) + 0.5, np.arange(n)) / n
    forward = np.concatenate([np.cos(angle), -np.sin(angle)])
    inverse = np.concatenate([np.cos(angle), -np.sin(angle)]).T[taps:] / taps
    fh, fl = split(forward)
    gh, gl = split(inverse / SCALE)
    return np.concatenate([fh, fl]), np.concatenate([gh, gl])


def conv_kernel(prev_ref, cur_ref, query_ref, w_ref, f_ref, g_ref, out_ref):
    f32 = jnp.float32
    half, taps = f_ref.shape[0] // 2, cur_ref.shape[1]
    dot = functools.partial(jnp.dot, preferred_element_type=f32)
    f = f_ref[...]
    window = jnp.concatenate([prev_ref[0], cur_ref[0]], axis=0)
    x = dot(f, window)
    x = x[:half] + x[half:]
    w = jnp.concatenate([w_ref[i] for i in range(w_ref.shape[0])], axis=1)
    w = w.reshape(-1, taps)
    wh = w.astype(jnp.bfloat16)
    wl = (w - wh.astype(f32)).astype(jnp.bfloat16)
    nt = functools.partial(
        lax.dot_general, dimension_numbers=(((1,), (1,)), ((), ())), preferred_element_type=f32
    )
    h = nt(f[:, :taps], wh)
    h = h[:half] + h[half:] + nt(f[:half, :taps], wl)
    xr, xi, hr, hi = x[:taps], x[taps:], h[:taps], h[taps:]
    p = jnp.concatenate([xr * hr - xi * hi, xr * hi + xi * hr], axis=0)
    ph = p.astype(jnp.bfloat16)
    plo = (p - ph.astype(f32)).astype(jnp.bfloat16)
    g = g_ref[...]
    y = dot(g, ph)
    y = y[:taps] + y[taps:] + dot(g[:taps], plo)
    out_ref[0] = (query_ref[0].astype(f32) * y).astype(out_ref.dtype)


def filtered_gate(prev, cur, query, taps, forward, inverse, shards):
    _, rows, channels = cur.shape
    own = channels // taps.shape[1]
    width = own * shards
    block = pl.BlockSpec((1, rows, width), lambda i: (0, 0, i))
    return pl.pallas_call(
        conv_kernel,
        grid=(channels // width,),
        in_specs=[
            block,
            block,
            block,
            pl.BlockSpec(taps.shape[:1] + (shards,) + taps.shape[2:], lambda i: (0, i, 0, 0)),
            pl.BlockSpec(forward.shape, lambda i: (0, 0)),
            pl.BlockSpec(inverse.shape, lambda i: (0, 0)),
        ],
        out_specs=block,
        out_shape=jax.ShapeDtypeStruct(cur.shape, jnp.bfloat16),
        name="filtered_gate",
    )(prev, cur, query, taps, forward, inverse)


def per_device(query_proj, key_proj, value_proj, filters):
    f32 = jnp.float32
    peers, steps = lax.axis_size("fsdp"), lax.axis_size("seq")
    own, taps = filters.shape
    part = own // steps
    mine = lax.dynamic_slice_in_dim(filters, lax.axis_index("seq") * part, part, 0)
    mine = (mine * SCALE).astype(WIRE)
    mine = jnp.broadcast_to(mine, (peers, part, taps))
    got = lax.all_to_all(mine, "fsdp", 0, 0, tiled=True)
    got = jnp.broadcast_to(got, (steps,) + got.shape)
    every = lax.all_to_all(got, "seq", 0, 0, tiled=True)
    mixed = (key_proj.astype(f32) * value_proj.astype(f32)).astype(jnp.bfloat16)
    earlier = lax.ppermute(mixed, "seq", [(i, i + 1) for i in range(steps - 1)])
    forward, inverse = transforms(taps)
    every = every.reshape(steps, peers, part, taps).astype(f32)
    return filtered_gate(earlier, mixed, query_proj, every, forward, inverse, 16)


def solution(mesh):
    rows = P("fsdp", "seq", None)
    return jax.shard_map(
        per_device,
        mesh=mesh,
        in_specs=(rows, rows, rows, P("fsdp", None)),
        out_specs=rows,
        check_vma=False,
    )
```

```python
import functools

import jax
import jax.numpy as jnp
import numpy as np
from jax import lax
from jax.experimental import pallas as pl
from jax.experimental.pallas import tpu as pltpu
from jax.sharding import PartitionSpec as P

WIRE = jnp.float16
SCALE = 4096.0

dot = functools.partial(jnp.dot, preferred_element_type=jnp.float32)
dot_rows = functools.partial(
    lax.dot_general, dimension_numbers=(((1,), (1,)), ((), ())), preferred_element_type=jnp.float32
)


def split(x):
    x = np.asarray(x, np.float32)
    hi = x.astype(jnp.bfloat16)
    return hi, (x - hi.astype(np.float32)).astype(jnp.bfloat16)


def transforms(taps):
    n = 2 * taps
    angle = 2 * np.pi * np.outer(np.arange(taps) + 0.5, np.arange(n)) / n
    forward = np.concatenate([np.cos(angle), -np.sin(angle)])
    fh, fl = split(forward)
    gh, gl = split(forward.T[taps:] / (taps * SCALE))
    head, tail = fh[:, :taps], fl[:, :taps]
    return (
        np.concatenate([fh, fl], axis=1),
        np.concatenate([head, head, tail], axis=1),
        np.concatenate([gh, gh, gl], axis=1),
    )


def spectrum_kernel(prev_ref, cur_ref, f_ref, x_ref):
    window = jnp.concatenate([prev_ref[0], cur_ref[0]], axis=0)
    x_ref[...] = dot(f_ref[...], jnp.concatenate([window, window], axis=0))


def gate_kernel(odd_ref, x_ref, mine_ref, other_ref, query_ref, f_ref, g_ref, out_ref):
    f32, bf16 = jnp.float32, jnp.bfloat16
    taps = mine_ref.shape[-1]
    odd = odd_ref[0] == 1
    mine, other = mine_ref[...], other_ref[...]
    w = jnp.concatenate([jnp.where(odd, other, mine), jnp.where(odd, mine, other)], axis=1)
    w = w.reshape(-1, taps)
    wh = w.astype(bf16)
    wl = (w - wh.astype(f32)).astype(bf16)
    h = dot_rows(f_ref[...], jnp.concatenate([wh, wl, wh], axis=1))
    xr, xi, hr, hi = x_ref[:taps], x_ref[taps:], h[:taps], h[taps:]
    p = jnp.concatenate([xr * hr - xi * hi, xr * hi + xi * hr], axis=0)
    ph = p.astype(bf16)
    low = (p - ph.astype(f32)).astype(bf16)
    y = dot(g_ref[...], jnp.concatenate([ph, low, ph], axis=0))
    out_ref[0] = (query_ref[0].astype(f32) * y).astype(out_ref.dtype)


VMEM = pl.BlockSpec(memory_space=pltpu.VMEM)
PARAMS = pltpu.CompilerParams(vmem_limit_bytes=24 << 20)


def spectrum(prev, cur, forward):
    return pl.pallas_call(
        spectrum_kernel,
        in_specs=[VMEM] * 3,
        out_specs=VMEM,
        out_shape=jax.ShapeDtypeStruct((forward.shape[0], cur.shape[2]), jnp.float32),
        compiler_params=PARAMS,
        name="spectrum",
    )(prev, cur, forward)


def gate(odd, x, mine, other, query, forward, inverse):
    return pl.pallas_call(
        gate_kernel,
        in_specs=[pl.BlockSpec(memory_space=pltpu.SMEM)] + [VMEM] * 6,
        out_specs=VMEM,
        out_shape=jax.ShapeDtypeStruct(query.shape, jnp.bfloat16),
        compiler_params=PARAMS,
        name="gate",
    )(odd, x, mine, other, query, forward, inverse)


def per_device(query_proj, key_proj, value_proj, filters):
    f32 = jnp.float32
    peers, steps = lax.axis_size("fsdp"), lax.axis_size("seq")
    own, taps = filters.shape
    window_dft, taps_dft, inverse = transforms(taps)
    mixed = (key_proj.astype(f32) * value_proj.astype(f32)).astype(jnp.bfloat16)
    earlier = lax.ppermute(mixed, "seq", [(i, i + 1) for i in range(steps - 1)])
    halves = (filters * SCALE).astype(WIRE).reshape(1, 2, own // 2, taps)
    send = jnp.broadcast_to(halves, (peers // 2, 2, own // 2, taps))
    mine = lax.all_to_all(send.reshape(peers, own // 2, taps), "fsdp", 0, 0, tiled=True)
    x = spectrum(earlier, mixed, window_dft)
    other = lax.ppermute(mine, "fsdp", [(i, i ^ 1) for i in range(peers)])
    mine = mine.astype(f32)
    odd = (lax.axis_index("fsdp") % 2).astype(jnp.int32).reshape(1)
    return gate(odd, x, mine, other.astype(f32), query_proj, taps_dft, inverse)


def solution(mesh):
    rows = P("fsdp", "seq", None)
    return jax.shard_map(
        per_device,
        mesh=mesh,
        in_specs=(rows, rows, rows, P("fsdp", None)),
        out_specs=rows,
        check_vma=False,
    )
```

```python
import functools

import jax
import jax.numpy as jnp
import numpy as np
from jax import lax
from jax.experimental import pallas as pl
from jax.experimental.pallas import tpu as pltpu
from jax.sharding import PartitionSpec as P

WIRE = jnp.float16
SCALE = 4096.0

dot = functools.partial(jnp.dot, preferred_element_type=jnp.float32)
dot_rows = functools.partial(
    lax.dot_general, dimension_numbers=(((1,), (1,)), ((), ())), preferred_element_type=jnp.float32
)


def split(x):
    x = np.asarray(x, np.float32)
    hi = x.astype(jnp.bfloat16)
    return hi, (x - hi.astype(np.float32)).astype(jnp.bfloat16)


def transforms(taps):
    n = 2 * taps
    angle = 2 * np.pi * np.outer(np.arange(taps) + 0.5, np.arange(n)) / n
    forward = np.concatenate([np.cos(angle), -np.sin(angle)])
    fh, fl = split(forward)
    gh, gl = split(forward.T[taps:] / (taps * SCALE))
    head, tail = fh[:, :taps], fl[:, :taps]
    return (
        np.concatenate([fh, fl], axis=1),
        np.block([[head, head], [tail, np.zeros_like(tail)]]),
        np.concatenate([gh, gl], axis=0),
    )


def spectrum_kernel(prev_ref, key_ref, value_ref, f_ref, x_ref):
    f32 = jnp.float32
    mixed = (key_ref[0].astype(f32) * value_ref[0].astype(f32)).astype(jnp.bfloat16)
    window = jnp.concatenate([prev_ref[0], mixed], axis=0)
    x_ref[...] = dot(f_ref[...], jnp.concatenate([window, window], axis=0))


def gate_kernel(x_ref, w_ref, query_ref, f_ref, g_ref, out_ref):
    f32, bf16 = jnp.float32, jnp.bfloat16
    steps, peers, part, taps = w_ref.shape
    w = jnp.concatenate([w_ref[i] for i in range(steps)], axis=1)
    w = w.reshape(steps * peers * part, taps)
    wh = w.astype(bf16)
    wl = (w - wh.astype(f32)).astype(bf16)
    h = dot_rows(f_ref[...], jnp.concatenate([wh, wl], axis=1))
    h = h[: 2 * taps] + h[2 * taps :]
    xr, xi, hr, hi = x_ref[:taps], x_ref[taps:], h[:taps], h[taps:]
    p = jnp.concatenate([xr * hr - xi * hi, xr * hi + xi * hr], axis=0)
    ph = p.astype(bf16)
    low = (p - ph.astype(f32)).astype(bf16)
    y = dot(g_ref[...], ph)
    y = y[:taps] + y[taps:] + dot(g_ref[:taps], low)
    out_ref[0] = (query_ref[0].astype(f32) * y).astype(out_ref.dtype)


VMEM = pl.BlockSpec(memory_space=pltpu.VMEM)
PARAMS = pltpu.CompilerParams(vmem_limit_bytes=24 << 20)


def spectrum(prev, key, value, forward):
    return pl.pallas_call(
        spectrum_kernel,
        in_specs=[VMEM] * 4,
        out_specs=VMEM,
        out_shape=jax.ShapeDtypeStruct((forward.shape[0], key.shape[2]), jnp.float32),
        compiler_params=PARAMS,
        name="spectrum",
    )(prev, key, value, forward)


def gate(x, w, query, forward, inverse):
    return pl.pallas_call(
        gate_kernel,
        in_specs=[VMEM] * 5,
        out_specs=VMEM,
        out_shape=jax.ShapeDtypeStruct(query.shape, jnp.bfloat16),
        compiler_params=PARAMS,
        name="gate",
    )(x, w, query, forward, inverse)


def per_device(query_proj, key_proj, value_proj, filters):
    f32 = jnp.float32
    peers, steps = lax.axis_size("fsdp"), lax.axis_size("seq")
    own, taps = filters.shape
    part = own // steps
    window_dft, taps_dft, inverse = transforms(taps)
    mixed = (key_proj.astype(f32) * value_proj.astype(f32)).astype(jnp.bfloat16)
    earlier = lax.ppermute(mixed, "seq", [(i, i + 1) for i in range(steps - 1)])
    mine = lax.dynamic_slice_in_dim(filters, lax.axis_index("seq") * part, part, 0)
    mine = (mine * SCALE).astype(WIRE)
    mine = jnp.broadcast_to(mine, (peers, part, taps))
    got = lax.all_to_all(mine, "fsdp", 0, 0, tiled=True)
    x = spectrum(earlier, key_proj, value_proj, window_dft)
    got = jnp.broadcast_to(got, (steps,) + got.shape)
    every = lax.all_to_all(got, "seq", 0, 0, tiled=True)
    every = every.reshape(steps, peers, part, taps).astype(f32)
    return gate(x, every, query_proj, taps_dft, inverse)


def solution(mesh):
    rows = P("fsdp", "seq", None)
    return jax.shard_map(
        per_device,
        mesh=mesh,
        in_specs=(rows, rows, rows, P("fsdp", None)),
        out_specs=rows,
        check_vma=False,
    )
```

```python
import functools

import jax
import jax.numpy as jnp
import numpy as np
from jax import lax
from jax.experimental import pallas as pl
from jax.experimental.pallas import tpu as pltpu
from jax.sharding import PartitionSpec as P

WIRE = jnp.float16
SCALE = 4096.0

dot = functools.partial(jnp.dot, preferred_element_type=jnp.float32)
dot_rows = functools.partial(
    lax.dot_general, dimension_numbers=(((1,), (1,)), ((), ())), preferred_element_type=jnp.float32
)


def split(x):
    x = np.asarray(x, np.float32)
    hi = x.astype(jnp.bfloat16)
    return hi, (x - hi.astype(np.float32)).astype(jnp.bfloat16)


def transforms(taps):
    n = 2 * taps
    angle = 2 * np.pi * np.outer(np.arange(taps) + 0.5, np.arange(n)) / n
    forward = np.concatenate([np.cos(angle), -np.sin(angle)])
    fh, fl = split(forward)
    gh, gl = split(forward.T[taps:] / (taps * SCALE))
    head, tail = fh[:, :taps], fl[:, :taps]
    return (
        np.concatenate([fh, fl], axis=1),
        np.block([[head, head], [tail, np.zeros_like(tail)]]),
        np.concatenate([gh, gl], axis=0),
    )


def spectrum_kernel(prev_ref, key_ref, value_ref, f_ref, x_ref):
    f32 = jnp.float32
    mixed = (key_ref[0].astype(f32) * value_ref[0].astype(f32)).astype(jnp.bfloat16)
    window = jnp.concatenate([prev_ref[0], mixed], axis=0)
    x_ref[...] = dot(f_ref[...], jnp.concatenate([window, window], axis=0))


def gate_kernel(odd_ref, x_ref, mine_ref, other_ref, query_ref, f_ref, g_ref, out_ref):
    f32, bf16 = jnp.float32, jnp.bfloat16
    taps = mine_ref.shape[-1]
    odd = odd_ref[0] == 1
    pieces = []
    for i in range(mine_ref.shape[0]):
        mine, other = mine_ref[i], other_ref[i]
        pieces += [jnp.where(odd, other, mine), jnp.where(odd, mine, other)]
    w = jnp.concatenate(pieces, axis=1).reshape(-1, taps)
    wh = w.astype(bf16)
    wl = (w - wh.astype(f32)).astype(bf16)
    h = dot_rows(f_ref[...], jnp.concatenate([wh, wl], axis=1))
    h = h[: 2 * taps] + h[2 * taps :]
    xr, xi, hr, hi = x_ref[:taps], x_ref[taps:], h[:taps], h[taps:]
    p = jnp.concatenate([xr * hr - xi * hi, xr * hi + xi * hr], axis=0)
    ph = p.astype(bf16)
    low = (p - ph.astype(f32)).astype(bf16)
    y = dot(g_ref[...], ph)
    y = y[:taps] + y[taps:] + dot(g_ref[:taps], low)
    out_ref[0] = (query_ref[0].astype(f32) * y).astype(out_ref.dtype)


VMEM = pl.BlockSpec(memory_space=pltpu.VMEM)
PARAMS = pltpu.CompilerParams(vmem_limit_bytes=24 << 20)


def spectrum(prev, key, value, forward):
    return pl.pallas_call(
        spectrum_kernel,
        in_specs=[VMEM] * 4,
        out_specs=VMEM,
        out_shape=jax.ShapeDtypeStruct((forward.shape[0], key.shape[2]), jnp.float32),
        compiler_params=PARAMS,
        name="spectrum",
    )(prev, key, value, forward)


def gate(odd, x, mine, other, query, forward, inverse):
    return pl.pallas_call(
        gate_kernel,
        in_specs=[pl.BlockSpec(memory_space=pltpu.SMEM)] + [VMEM] * 6,
        out_specs=VMEM,
        out_shape=jax.ShapeDtypeStruct(query.shape, jnp.bfloat16),
        compiler_params=PARAMS,
        name="gate",
    )(odd, x, mine, other, query, forward, inverse)


NEAR = 4


def stage_groups(peers):
    index = np.arange(peers).reshape(-1, NEAR, 2)
    far = [index[:, near, core].tolist() for near in range(NEAR) for core in range(2)]
    near = [index[chunk, :, core].tolist() for chunk in range(index.shape[0]) for core in range(2)]
    return far, near


def exchange(piece, groups):
    copies = jnp.broadcast_to(piece, (len(groups[0]),) + piece.shape)
    return lax.all_to_all(copies, "fsdp", 0, 0, axis_index_groups=groups, tiled=True)


def per_device(query_proj, key_proj, value_proj, filters):
    f32 = jnp.float32
    peers, steps = lax.axis_size("fsdp"), lax.axis_size("seq")
    window_dft, taps_dft, inverse = transforms(filters.shape[1])
    far, near = stage_groups(peers)
    mine = exchange((filters * SCALE).astype(WIRE), far)
    mixed = (key_proj.astype(f32) * value_proj.astype(f32)).astype(jnp.bfloat16)
    earlier = lax.ppermute(mixed, "seq", [(i, i + 1) for i in range(steps - 1)])
    mine = exchange(mine, near)
    x = spectrum(earlier, key_proj, value_proj, window_dft)
    other = lax.ppermute(mine, "fsdp", [(i, i ^ 1) for i in range(peers)])
    mine = mine.astype(f32)
    odd = (lax.axis_index("fsdp") % 2).astype(jnp.int32).reshape(1)
    return gate(odd, x, mine, other.astype(f32), query_proj, taps_dft, inverse)


def solution(mesh):
    rows = P("fsdp", "seq", None)
    return jax.shard_map(
        per_device,
        mesh=mesh,
        in_specs=(rows, rows, rows, P("fsdp", None)),
        out_specs=rows,
        check_vma=False,
    )
```

```python
import functools

import jax
import jax.numpy as jnp
import numpy as np
from jax import lax
from jax.experimental import pallas as pl
from jax.experimental.pallas import tpu as pltpu
from jax.sharding import PartitionSpec as P

WIRE = jnp.float16
SCALE = 4096.0

dot = functools.partial(jnp.dot, preferred_element_type=jnp.float32)
dot_rows = functools.partial(
    lax.dot_general, dimension_numbers=(((1,), (1,)), ((), ())), preferred_element_type=jnp.float32
)


def split(x):
    x = np.asarray(x, np.float32)
    hi = x.astype(jnp.bfloat16)
    return hi, (x - hi.astype(np.float32)).astype(jnp.bfloat16)


def transforms(taps):
    n = 2 * taps
    angle = 2 * np.pi * np.outer(np.arange(taps) + 0.5, np.arange(n)) / n
    forward = np.concatenate([np.cos(angle), -np.sin(angle)])
    fh, fl = split(forward)
    gh, gl = split(forward.T[taps:] / (taps * SCALE))
    head, tail = fh[:, :taps], fl[:, :taps]
    return (
        np.concatenate([fh, fl], axis=1),
        np.block([[head, head], [tail, np.zeros_like(tail)]]),
        np.concatenate([gh, gl], axis=0),
    )


def spectrum_kernel(prev_ref, key_ref, value_ref, f_ref, x_ref, prev, key, value, sems):
    copies = [
        pltpu.make_async_copy(source, target, sems.at[i])
        for i, (source, target) in enumerate(((key_ref, key), (value_ref, value), (prev_ref, prev)))
    ]
    for copy in copies:
        copy.start()
    for copy in copies:
        copy.wait()
    f32 = jnp.float32
    mixed = (key[0].astype(f32) * value[0].astype(f32)).astype(jnp.bfloat16)
    window = jnp.concatenate([prev[0], mixed], axis=0)
    x_ref[...] = dot(f_ref[...], jnp.concatenate([window, window], axis=0))


def gate_kernel(odd_ref, x_ref, mine_ref, other_ref, query_ref, f_ref, g_ref, out_ref):
    f32, bf16 = jnp.float32, jnp.bfloat16
    taps = mine_ref.shape[-1]
    odd = odd_ref[0] == 1
    pieces = []
    for i in range(mine_ref.shape[0]):
        mine, other = mine_ref[i], other_ref[i]
        pieces += [jnp.where(odd, other, mine), jnp.where(odd, mine, other)]
    w = jnp.concatenate(pieces, axis=1).reshape(-1, taps)
    wh = w.astype(bf16)
    wl = (w - wh.astype(f32)).astype(bf16)
    h = dot_rows(f_ref[...], jnp.concatenate([wh, wl], axis=1))
    h = h[: 2 * taps] + h[2 * taps :]
    xr, xi, hr, hi = x_ref[:taps], x_ref[taps:], h[:taps], h[taps:]
    p = jnp.concatenate([xr * hr - xi * hi, xr * hi + xi * hr], axis=0)
    ph = p.astype(bf16)
    low = (p - ph.astype(f32)).astype(bf16)
    y = dot(g_ref[...], ph)
    y = y[:taps] + y[taps:] + dot(g_ref[:taps], low)
    out_ref[0] = (query_ref[0].astype(f32) * y).astype(out_ref.dtype)


VMEM = pl.BlockSpec(memory_space=pltpu.VMEM)
PARAMS = pltpu.CompilerParams(vmem_limit_bytes=24 << 20)


def spectrum(prev, key, value, forward):
    return pl.pallas_call(
        spectrum_kernel,
        in_specs=[pl.BlockSpec(memory_space=pl.ANY)] * 3 + [VMEM],
        out_specs=VMEM,
        out_shape=jax.ShapeDtypeStruct((forward.shape[0], key.shape[2]), jnp.float32),
        scratch_shapes=[pltpu.VMEM(key.shape, key.dtype)] * 3 + [pltpu.SemaphoreType.DMA((3,))],
        compiler_params=PARAMS,
        name="spectrum",
    )(prev, key, value, forward)


def gate(odd, x, mine, other, query, forward, inverse):
    return pl.pallas_call(
        gate_kernel,
        in_specs=[pl.BlockSpec(memory_space=pltpu.SMEM)] + [VMEM] * 6,
        out_specs=VMEM,
        out_shape=jax.ShapeDtypeStruct(query.shape, jnp.bfloat16),
        compiler_params=PARAMS,
        name="gate",
    )(odd, x, mine, other, query, forward, inverse)


NEAR = 4


def stage_groups(peers):
    index = np.arange(peers).reshape(-1, NEAR, 2)
    far = [index[:, near, core].tolist() for near in range(NEAR) for core in range(2)]
    near = [index[chunk, :, core].tolist() for chunk in range(index.shape[0]) for core in range(2)]
    return far, near


def exchange(copies, groups):
    return lax.all_to_all(copies, "fsdp", 0, 0, axis_index_groups=groups, tiled=True)


def per_device(query_proj, key_proj, value_proj, filters):
    f32 = jnp.float32
    peers, steps = lax.axis_size("fsdp"), lax.axis_size("seq")
    window_dft, taps_dft, inverse = transforms(filters.shape[1])
    far, near = stage_groups(peers)
    copy = lax.broadcasted_iota(jnp.int32, (len(far[0]),) + filters.shape, 0)
    scale = SCALE + jnp.minimum(copy, 0).astype(f32)
    mine = exchange((filters[None] * scale).astype(WIRE), far)
    mixed = (key_proj.astype(f32) * value_proj.astype(f32)).astype(jnp.bfloat16)
    earlier = lax.ppermute(mixed, "seq", [(i, i + 1) for i in range(steps - 1)])
    mine = exchange(jnp.broadcast_to(mine, (NEAR,) + mine.shape), near)
    x = spectrum(earlier, key_proj, value_proj, window_dft)
    other = lax.ppermute(mine, "fsdp", [(i, i ^ 1) for i in range(peers)])
    mine = mine.astype(f32)
    odd = (lax.axis_index("fsdp") % 2).astype(jnp.int32).reshape(1)
    return gate(odd, x, mine, other.astype(f32), query_proj, taps_dft, inverse)


def solution(mesh):
    rows = P("fsdp", "seq", None)
    return jax.shard_map(
        per_device,
        mesh=mesh,
        in_specs=(rows, rows, rows, P("fsdp", None)),
        out_specs=rows,
        check_vma=False,
    )
```

```python
import functools

import jax
import jax.numpy as jnp
import numpy as np
from jax import lax
from jax.experimental import pallas as pl
from jax.experimental.pallas import tpu as pltpu
from jax.sharding import PartitionSpec as P

WIRE = jnp.float16
SCALE = 4096.0

dot = functools.partial(jnp.dot, preferred_element_type=jnp.float32)
dot_rows = functools.partial(
    lax.dot_general, dimension_numbers=(((1,), (1,)), ((), ())), preferred_element_type=jnp.float32
)


def split(x):
    x = np.asarray(x, np.float32)
    hi = x.astype(jnp.bfloat16)
    return hi, (x - hi.astype(np.float32)).astype(jnp.bfloat16)


def transforms(taps):
    n = 2 * taps
    angle = 2 * np.pi * np.outer(np.arange(taps) + 0.5, np.arange(n)) / n
    forward = np.concatenate([np.cos(angle), -np.sin(angle)])
    fh, fl = split(forward)
    gh, gl = split(forward.T[taps:] / (taps * SCALE))
    head, tail = fh[:, :taps], fl[:, :taps]
    return (
        np.concatenate([fh, fl], axis=1),
        np.block([[head, head], [tail, np.zeros_like(tail)]]),
        np.concatenate([gh, gl], axis=0),
    )


NEAR = 4
CHUNKS = 3


def near_order(members):
    return [members // 2] + [i for i in range(members) if i != members // 2]


def far_order(members):
    rows = members // CHUNKS
    return sorted(range(members), key=lambda i: (-(i % CHUNKS), (i // CHUNKS - rows // 2) % rows))


def stage_groups(peers):
    index = np.arange(peers).reshape(-1, NEAR, 2)
    chunks = index.shape[0]
    far = [index[far_order(chunks), near, core].tolist() for near in range(NEAR) for core in range(2)]
    near = [index[chunk, near_order(NEAR), core].tolist() for chunk in range(chunks) for core in range(2)]
    return far, near


def spectrum_kernel(prev_ref, cur_ref, query_ref, f_ref, x_ref, kept_ref, prev, cur, sems):
    pairs = ((cur_ref, cur), (prev_ref, prev), (query_ref, kept_ref))
    copies = [pltpu.make_async_copy(source, target, sems.at[i]) for i, (source, target) in enumerate(pairs)]
    for copy in copies:
        copy.start()
    for copy in copies[:2]:
        copy.wait()
    window = jnp.concatenate([prev[0], cur[0]], axis=0)
    x_ref[...] = dot(f_ref[...], jnp.concatenate([window, window], axis=0))
    copies[2].wait()


def gate_kernel(odd_ref, x_ref, mine_ref, other_ref, query_ref, f_ref, g_ref, out_ref):
    f32, bf16 = jnp.float32, jnp.bfloat16
    near, far, _, taps = mine_ref.shape
    odd = odd_ref[0] == 1
    pieces = []
    for i in range(near):
        at = near_order(near).index(i)
        for ref, twin in ((mine_ref, other_ref), (other_ref, mine_ref)):
            piece = jnp.where(odd, twin[at], ref[at])
            pieces.append(jnp.stack([piece[far_order(far).index(j)] for j in range(far)]))
    w = jnp.concatenate(pieces, axis=1).reshape(-1, taps)
    wh = w.astype(bf16)
    wl = (w - wh.astype(f32)).astype(bf16)
    h = dot_rows(f_ref[...], jnp.concatenate([wh, wl], axis=1))
    h = h[: 2 * taps] + h[2 * taps :]
    xr, xi, hr, hi = x_ref[:taps], x_ref[taps:], h[:taps], h[taps:]
    p = jnp.concatenate([xr * hr - xi * hi, xr * hi + xi * hr], axis=0)
    ph = p.astype(bf16)
    low = (p - ph.astype(f32)).astype(bf16)
    y = dot(g_ref[...], ph)
    y = y[:taps] + y[taps:] + dot(g_ref[:taps], low)
    out_ref[0] = (query_ref[0].astype(f32) * y).astype(out_ref.dtype)


VMEM = pl.BlockSpec(memory_space=pltpu.VMEM)
PARAMS = pltpu.CompilerParams(vmem_limit_bytes=24 << 20)


def spectrum(prev, cur, query, forward):
    x = jax.ShapeDtypeStruct((forward.shape[0], cur.shape[2]), jnp.float32)
    return pl.pallas_call(
        spectrum_kernel,
        in_specs=[pl.BlockSpec(memory_space=pl.ANY)] * 3 + [VMEM],
        out_specs=[VMEM] * 2,
        out_shape=[x, jax.ShapeDtypeStruct(query.shape, query.dtype)],
        scratch_shapes=[pltpu.VMEM(cur.shape, cur.dtype)] * 2 + [pltpu.SemaphoreType.DMA((3,))],
        compiler_params=PARAMS,
        name="spectrum",
    )(prev, cur, query, forward)


def gate(odd, x, mine, other, query, forward, inverse):
    return pl.pallas_call(
        gate_kernel,
        in_specs=[pl.BlockSpec(memory_space=pltpu.SMEM)] + [VMEM] * 6,
        out_specs=VMEM,
        out_shape=jax.ShapeDtypeStruct(query.shape, jnp.bfloat16),
        compiler_params=PARAMS,
        name="gate",
    )(odd, x, mine, other, query, forward, inverse)


def exchange(copies, groups):
    return lax.all_to_all(copies, "fsdp", 0, 0, axis_index_groups=groups, tiled=True)


def per_device(query_proj, key_proj, value_proj, filters):
    f32 = jnp.float32
    peers, steps = lax.axis_size("fsdp"), lax.axis_size("seq")
    window_dft, taps_dft, inverse = transforms(filters.shape[1])
    far, near = stage_groups(peers)
    mine = (filters * SCALE).astype(WIRE)
    mine = exchange(jnp.broadcast_to(mine, (len(far[0]),) + mine.shape), far)
    mixed = (key_proj.astype(f32) * value_proj.astype(f32)).astype(jnp.bfloat16)
    earlier = lax.ppermute(mixed, "seq", [(i, i + 1) for i in range(steps - 1)])
    mine = exchange(jnp.broadcast_to(mine, (NEAR,) + mine.shape), near)
    x, query = spectrum(earlier, mixed, query_proj, window_dft)
    other = lax.ppermute(mine, "fsdp", [(i, i ^ 1) for i in range(peers)])
    mine = mine.astype(f32)
    odd = (lax.axis_index("fsdp") % 2).astype(jnp.int32).reshape(1)
    return gate(odd, x, mine, other.astype(f32), query, taps_dft, inverse)


def solution(mesh):
    rows = P("fsdp", "seq", None)
    return jax.shard_map(
        per_device,
        mesh=mesh,
        in_specs=(rows, rows, rows, P("fsdp", None)),
        out_specs=rows,
        check_vma=False,
    )
```

```python
import functools

import jax
import jax.numpy as jnp
import numpy as np
from jax import lax
from jax.experimental import pallas as pl
from jax.experimental.pallas import tpu as pltpu
from jax.sharding import PartitionSpec as P

WIRE = jnp.float16
SCALE = 4096.0

dot = functools.partial(jnp.dot, preferred_element_type=jnp.float32)
dot_rows = functools.partial(
    lax.dot_general, dimension_numbers=(((1,), (1,)), ((), ())), preferred_element_type=jnp.float32
)


def split(x):
    x = np.asarray(x, np.float32)
    hi = x.astype(jnp.bfloat16)
    return hi, (x - hi.astype(np.float32)).astype(jnp.bfloat16)


def transforms(taps):
    n = 2 * taps
    angle = 2 * np.pi * np.outer(np.arange(taps) + 0.5, np.arange(n)) / n
    forward = np.concatenate([np.cos(angle), -np.sin(angle)])
    fh, fl = split(forward)
    gh, gl = split(forward.T[taps:] / (taps * SCALE))
    head, tail = fh[:, :taps], fl[:, :taps]
    return (
        np.concatenate([head, tail], axis=1),
        np.concatenate([fh[:, taps:], fl[:, taps:]], axis=1),
        np.block([[head, head], [tail, np.zeros_like(tail)]]),
        np.concatenate([gh, gl], axis=0),
    )


NEAR = 4
CHUNKS = 3


def near_order(members):
    return [members // 2] + [i for i in range(members) if i != members // 2]


def far_order(members):
    rows = members // CHUNKS
    return sorted(range(members), key=lambda i: (-(i % CHUNKS), (i // CHUNKS - rows // 2) % rows))


def stage_groups(peers):
    index = np.arange(peers).reshape(-1, NEAR, 2)
    chunks = index.shape[0]
    far = [index[far_order(chunks), near, core].tolist() for near in range(NEAR) for core in range(2)]
    near = [index[chunk, near_order(NEAR), core].tolist() for chunk in range(chunks) for core in range(2)]
    return far, near


def twice(x):
    return jnp.concatenate([x, x], axis=0)


def spectrum_kernel(cur_ref, query_ref, f_ref, x_ref, kept_ref, cur, sems):
    pairs = ((cur_ref, cur), (query_ref, kept_ref))
    copies = [pltpu.make_async_copy(source, target, sems.at[i]) for i, (source, target) in enumerate(pairs)]
    for copy in copies:
        copy.start()
    copies[0].wait()
    x_ref[...] = dot(f_ref[...], twice(cur[0]))
    copies[1].wait()


BLOCKS = 2


def gate_kernel(odd_ref, x_ref, prev_ref, mine_ref, other_ref, query_ref, d_ref, f_ref, g_ref, out_ref, prev, sem):
    copy = pltpu.make_async_copy(prev_ref, prev, sem)
    copy.start()
    f32, bf16 = jnp.float32, jnp.bfloat16
    near, far, _, taps = mine_ref.shape
    odd = odd_ref[0] == 1
    copy.wait()
    for block in range(BLOCKS):
        members = range(block * far // BLOCKS, (block + 1) * far // BLOCKS)
        width = query_ref.shape[2] // BLOCKS
        at = slice(block * width, (block + 1) * width)
        pieces = []
        for i in range(near):
            i = near_order(near).index(i)
            for ref, twin in ((mine_ref, other_ref), (other_ref, mine_ref)):
                chosen = [far_order(far).index(j) for j in members]
                pieces.append(jnp.stack([jnp.where(odd, twin[i, j], ref[i, j]) for j in chosen]))
        w = jnp.concatenate(pieces, axis=1).reshape(-1, taps)
        wh = w.astype(bf16)
        wl = (w - wh.astype(f32)).astype(bf16)
        h = dot_rows(f_ref[...], jnp.concatenate([wh, wl], axis=1))
        h = h[: 2 * taps] + h[2 * taps :]
        x = x_ref[:, at] + dot(d_ref[...], twice(prev[0, :, at]))
        xr, xi, hr, hi = x[:taps], x[taps:], h[:taps], h[taps:]
        p = jnp.concatenate([xr * hr - xi * hi, xr * hi + xi * hr], axis=0)
        ph = p.astype(bf16)
        low = (p - ph.astype(f32)).astype(bf16)
        y = dot(g_ref[...], ph)
        y = y[:taps] + y[taps:] + dot(g_ref[:taps], low)
        out_ref[0, :, at] = (query_ref[0, :, at].astype(f32) * y).astype(out_ref.dtype)


VMEM = pl.BlockSpec(memory_space=pltpu.VMEM)
ANY = pl.BlockSpec(memory_space=pl.ANY)
PARAMS = pltpu.CompilerParams(vmem_limit_bytes=24 << 20)


def spectrum(cur, query, forward):
    x = jax.ShapeDtypeStruct((forward.shape[0], cur.shape[2]), jnp.float32)
    return pl.pallas_call(
        spectrum_kernel,
        in_specs=[ANY] * 2 + [VMEM],
        out_specs=[VMEM] * 2,
        out_shape=[x, jax.ShapeDtypeStruct(query.shape, query.dtype)],
        scratch_shapes=[pltpu.VMEM(cur.shape, cur.dtype), pltpu.SemaphoreType.DMA((2,))],
        compiler_params=PARAMS,
        name="spectrum",
    )(cur, query, forward)


def gate(odd, x, prev, mine, other, query, earlier, forward, inverse):
    return pl.pallas_call(
        gate_kernel,
        in_specs=[pl.BlockSpec(memory_space=pltpu.SMEM), VMEM, ANY] + [VMEM] * 6,
        out_specs=VMEM,
        out_shape=jax.ShapeDtypeStruct(query.shape, jnp.bfloat16),
        scratch_shapes=[pltpu.VMEM(prev.shape, prev.dtype), pltpu.SemaphoreType.DMA],
        compiler_params=PARAMS,
        name="gate",
    )(odd, x, prev, mine, other, query, earlier, forward, inverse)


def exchange(copies, groups):
    return lax.all_to_all(copies, "fsdp", 0, 0, axis_index_groups=groups, tiled=True)


def per_device(query_proj, key_proj, value_proj, filters):
    f32 = jnp.float32
    peers, steps = lax.axis_size("fsdp"), lax.axis_size("seq")
    earlier_dft, own_dft, taps_dft, inverse = transforms(filters.shape[1])
    far, near = stage_groups(peers)
    mine = (filters * SCALE).astype(WIRE)
    mine = exchange(jnp.broadcast_to(mine, (len(far[0]),) + mine.shape), far)
    mixed = (key_proj.astype(f32) * value_proj.astype(f32)).astype(jnp.bfloat16)
    earlier = lax.ppermute(mixed, "seq", [(i, i + 1) for i in range(steps - 1)])
    x, query = spectrum(mixed, query_proj, own_dft)
    mine = exchange(jnp.broadcast_to(mine, (NEAR,) + mine.shape), near)
    other = lax.ppermute(mine, "fsdp", [(i, i ^ 1) for i in range(peers)])
    mine = mine.astype(f32)
    odd = (lax.axis_index("fsdp") % 2).astype(jnp.int32).reshape(1)
    return gate(odd, x, earlier, mine, other.astype(f32), query, earlier_dft, taps_dft, inverse)


def solution(mesh):
    rows = P("fsdp", "seq", None)
    return jax.shard_map(
        per_device,
        mesh=mesh,
        in_specs=(rows, rows, rows, P("fsdp", None)),
        out_specs=rows,
        check_vma=False,
    )
```

```python
import functools

import jax
import jax.numpy as jnp
import numpy as np
from jax import lax
from jax.experimental import pallas as pl
from jax.experimental.pallas import tpu as pltpu
from jax.sharding import PartitionSpec as P

WIRE = jnp.float16
SCALE = 4096.0

dot = functools.partial(jnp.dot, preferred_element_type=jnp.float32)
dot_rows = functools.partial(
    lax.dot_general, dimension_numbers=(((1,), (1,)), ((), ())), preferred_element_type=jnp.float32
)


def split(x):
    x = np.asarray(x, np.float32)
    hi = x.astype(jnp.bfloat16)
    return hi, (x - hi.astype(np.float32)).astype(jnp.bfloat16)


def transforms(taps):
    n = 2 * taps
    angle = 2 * np.pi * np.outer(np.arange(taps) + 0.5, np.arange(n)) / n
    forward = np.concatenate([np.cos(angle), -np.sin(angle)])
    fh, fl = split(forward)
    gh, gl = split(forward.T[taps:] / (taps * SCALE))
    head, tail = fh[:, :taps], fl[:, :taps]
    return (
        np.concatenate([head, tail], axis=1),
        np.concatenate([fh[:, taps:], fl[:, taps:]], axis=1),
        np.block([[head, head], [tail, np.zeros_like(tail)]]),
        np.concatenate([gh, gl], axis=0),
    )


NEAR = 4
CHUNKS = 3
LATE = 2


def near_order(members):
    return [members // 2] + [i for i in range(members) if i != members // 2]


def far_order(members):
    rows = members // CHUNKS
    return sorted(range(members), key=lambda i: ((i - LATE) % CHUNKS, (i // CHUNKS - rows // 2) % rows))


def stage_groups(peers):
    index = np.arange(peers).reshape(-1, NEAR, 2)
    chunks = index.shape[0]
    far = [index[far_order(chunks), near, core].tolist() for near in range(NEAR) for core in range(2)]
    near = [index[chunk, near_order(NEAR), core].tolist() for chunk in range(chunks) for core in range(2)]
    return far, near


def twice(x):
    return jnp.concatenate([x, x], axis=0)


EARLY = 4


def is_early(row):
    return (row // 2) % (NEAR * CHUNKS) < EARLY


def fetch(early, first_ref, second_ref, target, sem):
    copies = [pltpu.make_async_copy(source, target, sem) for source in (first_ref, second_ref)]
    pl.when(early)(copies[0].start)
    pl.when(jnp.logical_not(early))(copies[1].start)
    return copies[0]


def mix_kernel(run, row_ref, key_ref, value_ref, out_ref, key, value, sems):
    early = is_early(row_ref[0])

    @pl.when(early if run else jnp.logical_not(early))
    def _():
        f32 = jnp.float32
        copies = [pltpu.make_async_copy(key_ref, key, sems.at[0]), pltpu.make_async_copy(value_ref, value, sems.at[1])]
        for copy in copies:
            copy.start()
        for copy in copies:
            copy.wait()
        out_ref[...] = (key[...].astype(f32) * value[...].astype(f32)).astype(out_ref.dtype)


def spectrum_kernel(row_ref, first_ref, second_ref, *refs):
    count = (len(refs) - 4) // 2
    kept, (f_ref, x_ref), rest = refs[:count], refs[count : count + 2], refs[count + 2 :]
    copies_ref, (cur, sems) = rest[:count], rest[count:]
    own = fetch(is_early(row_ref[0]), first_ref, second_ref, cur, sems.at[count])
    copies = [pltpu.make_async_copy(kept[i], copies_ref[i], sems.at[i]) for i in range(count)]
    for copy in copies:
        copy.start()
    own.wait()
    x_ref[...] = dot(f_ref[...], twice(cur[0]))
    for copy in copies:
        copy.wait()


BLOCKS = 2


def gate_kernel(
    row_ref, x_ref, first_ref, second_ref, mine_ref, other_ref, query_ref, d_ref, f_ref, g_ref, out_ref, prev, done, sem, out_sems
):
    copy = fetch(is_early(row_ref[0]), first_ref, second_ref, prev, sem)
    f32, bf16 = jnp.float32, jnp.bfloat16
    near, far, _, taps = mine_ref.shape
    width = query_ref.shape[2] // BLOCKS
    odd = row_ref[0] % 2 == 1
    copy.wait()
    copies = []
    for block in range(BLOCKS):
        members = range(block * far // BLOCKS, (block + 1) * far // BLOCKS)
        at = slice(block * width, (block + 1) * width)
        pieces = []
        for i in range(near):
            i = near_order(near).index(i)
            for ref, twin in ((mine_ref, other_ref), (other_ref, mine_ref)):
                chosen = [far_order(far).index(j) for j in members]
                pieces.append(jnp.stack([jnp.where(odd, twin[i, j], ref[i, j]) for j in chosen]))
        w = jnp.concatenate(pieces, axis=1).reshape(-1, taps)
        wh = w.astype(bf16)
        wl = (w - wh.astype(f32)).astype(bf16)
        x = x_ref[:, at] + dot(d_ref[...], twice(prev[0, :, at]))
        h = dot_rows(f_ref[...], jnp.concatenate([wh, wl], axis=1))
        h = h[: 2 * taps] + h[2 * taps :]
        xr, xi, hr, hi = x[:taps], x[taps:], h[:taps], h[taps:]
        p = jnp.concatenate([xr * hr - xi * hi, xr * hi + xi * hr], axis=0)
        ph = p.astype(bf16)
        low = (p - ph.astype(f32)).astype(bf16)
        y = dot(g_ref[...], ph)
        y = y[:taps] + y[taps:] + dot(g_ref[:taps], low)
        done[0, :, at] = (query_ref[0, :, at].astype(f32) * y).astype(done.dtype)
        copies.append(pltpu.make_async_copy(done.at[:, :, at], out_ref.at[:, :, at], out_sems.at[block]))
        copies[-1].start()
    for copy in copies:
        copy.wait()


VMEM = pl.BlockSpec(memory_space=pltpu.VMEM)
ANY = pl.BlockSpec(memory_space=pl.ANY)
SMEM = pl.BlockSpec(memory_space=pltpu.SMEM)
PARAMS = pltpu.CompilerParams(vmem_limit_bytes=24 << 20)


def mix(run, row, key, value):
    return pl.pallas_call(
        functools.partial(mix_kernel, run),
        in_specs=[SMEM, ANY, ANY],
        out_specs=VMEM,
        out_shape=jax.ShapeDtypeStruct(key.shape, jnp.bfloat16),
        scratch_shapes=[pltpu.VMEM(key.shape, key.dtype)] * 2 + [pltpu.SemaphoreType.DMA((2,))],
        name="mix",
    )(row, key, value)


def spectrum(row, first, second, kept, forward):
    x = jax.ShapeDtypeStruct((forward.shape[0], first.shape[2]), jnp.float32)
    return pl.pallas_call(
        spectrum_kernel,
        in_specs=[SMEM] + [ANY] * (2 + len(kept)) + [VMEM],
        out_specs=[VMEM] * (1 + len(kept)),
        out_shape=[x] + [jax.ShapeDtypeStruct(a.shape, a.dtype) for a in kept],
        scratch_shapes=[pltpu.VMEM(first.shape, first.dtype), pltpu.SemaphoreType.DMA((1 + len(kept),))],
        compiler_params=PARAMS,
        name="spectrum",
    )(row, first, second, *kept, forward)


def gate(row, x, first, second, mine, other, query, earlier, forward, inverse):
    return pl.pallas_call(
        gate_kernel,
        in_specs=[SMEM, VMEM, ANY, ANY] + [VMEM] * 6,
        out_specs=ANY,
        out_shape=jax.ShapeDtypeStruct(query.shape, jnp.bfloat16),
        scratch_shapes=[pltpu.VMEM(query.shape, jnp.bfloat16)] * 2
        + [pltpu.SemaphoreType.DMA, pltpu.SemaphoreType.DMA((BLOCKS,))],
        compiler_params=PARAMS,
        name="gate",
    )(row, x, first, second, mine, other, query, earlier, forward, inverse)


def exchange(copies, groups):
    return lax.all_to_all(copies, "fsdp", 0, 0, axis_index_groups=groups, tiled=True)


def halo(mixed, rows, steps):
    pairs = [(row * steps + i, row * steps + i + 1) for row in rows for i in range(steps - 1)]
    return lax.ppermute(mixed, ("fsdp", "seq"), pairs)


def per_device(query_proj, key_proj, value_proj, filters):
    f32 = jnp.float32
    peers, steps = lax.axis_size("fsdp"), lax.axis_size("seq")
    earlier_dft, own_dft, taps_dft, inverse = transforms(filters.shape[1])
    far, near = stage_groups(peers)
    row = lax.axis_index("fsdp").astype(jnp.int32).reshape(1)
    early = [i for i in range(peers) if is_early(i)]
    late = [i for i in range(peers) if not is_early(i)]
    first = mix(True, row, key_proj, value_proj)
    first_halo = halo(first, early, steps)
    mine = (filters * SCALE).astype(WIRE)
    mine = exchange(jnp.broadcast_to(mine, (len(far[0]),) + mine.shape), far)
    second = mix(False, row, key_proj, value_proj)
    second_halo = halo(second, late, steps)
    mine = exchange(jnp.broadcast_to(mine, (NEAR,) + mine.shape), near)
    other = lax.ppermute(mine, "fsdp", [(i, i ^ 1) for i in range(peers)])
    x, query, taps_dft = spectrum(row, first, second, (query_proj, taps_dft), own_dft)
    mine = mine.astype(f32)
    other = other.astype(f32)
    return gate(row, x, first_halo, second_halo, mine, other, query, earlier_dft, taps_dft, inverse)


def solution(mesh):
    rows = P("fsdp", "seq", None)
    return jax.shard_map(
        per_device,
        mesh=mesh,
        in_specs=(rows, rows, rows, P("fsdp", None)),
        out_specs=rows,
        check_vma=False,
    )
```

```python
import functools

import jax
import jax.numpy as jnp
import numpy as np
from jax import lax
from jax.experimental import pallas as pl
from jax.experimental.pallas import tpu as pltpu
from jax.sharding import PartitionSpec as P

WIRE = jnp.float16
SCALE = 4096.0

dot = functools.partial(jnp.dot, preferred_element_type=jnp.float32)
dot_rows = functools.partial(
    lax.dot_general, dimension_numbers=(((1,), (1,)), ((), ())), preferred_element_type=jnp.float32
)


def split(x):
    x = np.asarray(x, np.float32)
    hi = x.astype(jnp.bfloat16)
    return hi, (x - hi.astype(np.float32)).astype(jnp.bfloat16)


def transforms(taps):
    n = 2 * taps
    angle = 2 * np.pi * np.outer(np.arange(taps) + 0.5, np.arange(n)) / n
    forward = np.concatenate([np.cos(angle), -np.sin(angle)])
    fh, fl = split(forward)
    gh, gl = split(forward.T[taps:] / (taps * SCALE))
    head, tail = fh[:, :taps], fl[:, :taps]
    return (
        np.concatenate([head, tail], axis=1),
        np.concatenate([fh[:, taps:], fl[:, taps:]], axis=1),
        np.block([[head, head], [tail, np.zeros_like(tail)]]),
        np.concatenate([gh, gl], axis=0),
    )


NEAR = 4
CHUNKS = 3
LATE = 2


def near_order(members):
    return [members // 2] + [i for i in range(members) if i != members // 2]


def far_order(members):
    rows = members // CHUNKS
    return sorted(range(members), key=lambda i: ((i - LATE) % CHUNKS, (i // CHUNKS - rows // 2) % rows))


def stage_groups(peers):
    index = np.arange(peers).reshape(-1, NEAR, 2)
    chunks = index.shape[0]
    far = [index[far_order(chunks), near, core].tolist() for near in range(NEAR) for core in range(2)]
    near = [index[chunk, near_order(NEAR), core].tolist() for chunk in range(chunks) for core in range(2)]
    return far, near


def twice(x):
    return jnp.concatenate([x, x], axis=0)


def spectrum_kernel(cur_ref, *refs):
    count = (len(refs) - 4) // 2
    kept, (f_ref, x_ref), rest = refs[:count], refs[count : count + 2], refs[count + 2 :]
    copies_ref, (cur, sems) = rest[:count], rest[count:]
    pairs = ((cur_ref, cur),) + tuple(zip(kept, copies_ref))
    copies = [pltpu.make_async_copy(source, target, sems.at[i]) for i, (source, target) in enumerate(pairs)]
    for copy in copies:
        copy.start()
    copies[0].wait()
    x_ref[...] = dot(f_ref[...], twice(cur[0]))
    for copy in copies[1:]:
        copy.wait()


BLOCKS = 2


def gate_kernel(
    odd_ref, x_ref, prev_ref, mine_ref, other_ref, query_ref, d_ref, f_ref, g_ref, out_ref, prev, done, sem, out_sems
):
    copy = pltpu.make_async_copy(prev_ref, prev, sem)
    copy.start()
    f32, bf16 = jnp.float32, jnp.bfloat16
    near, far, _, taps = mine_ref.shape
    width = query_ref.shape[2] // BLOCKS
    odd = odd_ref[0] == 1
    copy.wait()
    copies = []
    for block in range(BLOCKS):
        members = range(block * far // BLOCKS, (block + 1) * far // BLOCKS)
        at = slice(block * width, (block + 1) * width)
        pieces = []
        for i in range(near):
            i = near_order(near).index(i)
            for ref, twin in ((mine_ref, other_ref), (other_ref, mine_ref)):
                chosen = [far_order(far).index(j) for j in members]
                pieces.append(jnp.stack([jnp.where(odd, twin[i, j], ref[i, j]) for j in chosen]))
        w = jnp.concatenate(pieces, axis=1).reshape(-1, taps)
        wh = w.astype(bf16)
        wl = (w - wh.astype(f32)).astype(bf16)
        x = x_ref[:, at] + dot(d_ref[...], twice(prev[0, :, at]))
        h = dot_rows(f_ref[...], jnp.concatenate([wh, wl], axis=1))
        h = h[: 2 * taps] + h[2 * taps :]
        xr, xi, hr, hi = x[:taps], x[taps:], h[:taps], h[taps:]
        p = jnp.concatenate([xr * hr - xi * hi, xr * hi + xi * hr], axis=0)
        ph = p.astype(bf16)
        low = (p - ph.astype(f32)).astype(bf16)
        y = dot(g_ref[...], ph)
        y = y[:taps] + y[taps:] + dot(g_ref[:taps], low)
        done[0, :, at] = (query_ref[0, :, at].astype(f32) * y).astype(done.dtype)
        copies.append(pltpu.make_async_copy(done.at[:, :, at], out_ref.at[:, :, at], out_sems.at[block]))
        copies[-1].start()
    for copy in copies:
        copy.wait()


VMEM = pl.BlockSpec(memory_space=pltpu.VMEM)
ANY = pl.BlockSpec(memory_space=pl.ANY)
PARAMS = pltpu.CompilerParams(vmem_limit_bytes=24 << 20)


def spectrum(cur, kept, forward):
    x = jax.ShapeDtypeStruct((forward.shape[0], cur.shape[2]), jnp.float32)
    return pl.pallas_call(
        spectrum_kernel,
        in_specs=[ANY] * (1 + len(kept)) + [VMEM],
        out_specs=[VMEM] * (1 + len(kept)),
        out_shape=[x] + [jax.ShapeDtypeStruct(a.shape, a.dtype) for a in kept],
        scratch_shapes=[pltpu.VMEM(cur.shape, cur.dtype), pltpu.SemaphoreType.DMA((1 + len(kept),))],
        compiler_params=PARAMS,
        name="spectrum",
    )(cur, *kept, forward)


def gate(odd, x, prev, mine, other, query, earlier, forward, inverse):
    return pl.pallas_call(
        gate_kernel,
        in_specs=[pl.BlockSpec(memory_space=pltpu.SMEM), VMEM, ANY] + [VMEM] * 6,
        out_specs=ANY,
        out_shape=jax.ShapeDtypeStruct(query.shape, jnp.bfloat16),
        scratch_shapes=[pltpu.VMEM(query.shape, jnp.bfloat16)] * 2
        + [pltpu.SemaphoreType.DMA, pltpu.SemaphoreType.DMA((BLOCKS,))],
        compiler_params=PARAMS,
        name="gate",
    )(odd, x, prev, mine, other, query, earlier, forward, inverse)


def exchange(copies, groups):
    return lax.all_to_all(copies, "fsdp", 0, 0, axis_index_groups=groups, tiled=True)


def per_device(query_proj, key_proj, value_proj, filters):
    f32 = jnp.float32
    peers, steps = lax.axis_size("fsdp"), lax.axis_size("seq")
    earlier_dft, own_dft, taps_dft, inverse = transforms(filters.shape[1])
    far, near = stage_groups(peers)
    mine = (filters * SCALE).astype(WIRE)
    mine = exchange(jnp.broadcast_to(mine, (len(far[0]),) + mine.shape), far)
    mixed = (key_proj.astype(f32) * value_proj.astype(f32)).astype(jnp.bfloat16)
    earlier = lax.ppermute(mixed, "seq", [(i, i + 1) for i in range(steps - 1)])
    x, *kept = spectrum(mixed, (query_proj, taps_dft), own_dft)
    mine = exchange(jnp.broadcast_to(mine, (NEAR,) + mine.shape), near)
    other = lax.ppermute(mine, "fsdp", [(i, i ^ 1) for i in range(peers)])
    mine = mine.astype(f32)
    odd = (lax.axis_index("fsdp") % 2).astype(jnp.int32).reshape(1)
    return gate(odd, x, earlier, mine, other.astype(f32), kept[0], earlier_dft, kept[1], inverse)


def solution(mesh):
    rows = P("fsdp", "seq", None)
    return jax.shard_map(
        per_device,
        mesh=mesh,
        in_specs=(rows, rows, rows, P("fsdp", None)),
        out_specs=rows,
        check_vma=False,
    )
```
